128 devices in a mesh: grp: 8 (over z, core), ep: 16 (over x, y).
Axes of the slice: x: 4, y: 4, z: 4, core: 2. Of those that a mesh axis runs over, the one named last changes fastest.
Arguments:
- hidden_in: bfloat16 [16384, 2048], P(('grp', 'ep')), may hold values from -24 to 24
- prompt_lengths: int32 [8, 5], P('grp'), may hold values from 1 to 1024, 2048 in all within a row
- routes: int32 [16384, 6], P(('grp', 'ep')), may hold values from 0 to 63, all different within a row; in each aligned block of 128 rows (0 to 127, 128 to 255, ...) at most 16 rows name the same one
- route_weights: float32 [16384, 6], P(('grp', 'ep')), may hold values from 0.05 to 0.4
- w_query: bfloat16 [2048, 2048], P(None, 'ep'), may hold values from -3 to 3
- w_key: bfloat16 [2048, 2048], P(None, 'ep'), may hold values from -3 to 3
- w_value: bfloat16 [2048, 2048], P(None, 'ep'), may hold values from -0.125 to 0.125
- w_out: bfloat16 [2048, 2048], replicated, may hold values from -0.125 to 0.125
- shared_gate: bfloat16 [2048, 2816], P(None, 'grp'), may hold values from -0.125 to 0.125
- shared_up: bfloat16 [2048, 2816], P(None, 'grp'), may hold values from -0.125 to 0.125
- shared_down: bfloat16 [2816, 2048], P('grp'), may hold values from -0.109375 to 0.109375
- expert_gate: bfloat16 [128, 2048, 704], P(('grp', 'ep')), may hold values from -0.125 to 0.125
- expert_up: bfloat16 [128, 2048, 704], P(('grp', 'ep')), may hold values from -0.125 to 0.125
- expert_down: bfloat16 [128, 704, 2048], P(('grp', 'ep')), may hold values from -0.15625 to 0.15625
Outputs:
- attended: bfloat16 [16384, 2048], P(('grp', 'ep'))
- moe_update: bfloat16 [16384, 2048], P(('grp', 'ep'))
The draws below stay inside these ranges and needn't reach their ends.
Inputs may be any that keep to these rules, and one draw needn't show every extreme that they name: `routes`: each row names 6 different experts. The 128 rows of one device name any one expert at most 16 times, and in every draw some device names some expert exactly 16 times. `prompt_lengths`: row g describes group g: its first 4 entries are the lengths of the packed prompts in order, the last one the padding positions at the group's end. Each row sums to 2048, and its largest entry is 1024.
All inputs are finite; a program needn't handle non-finite values.
Results may differ from the reference program's by a relative error of at most 0.015.
The reference program's roundings to bfloat16 on the way count: a program that leaves them out, or rounds other values in their place, can miss the bound.
Values may be sent and summed in bfloat16 or wider, within the bound.
A program may use at most 128 MiB of HBM per device.

```python
import math
import jax
import jax.numpy as jnp
import numpy as np
from jax import lax

D = 2048
HEADS = 16
HDIM = 128
FF_E = 1408
SHARED_FF = 2816
TOPK = 6
TOK_DEV = 128
PROMPTS = 4
EXPERTS = 64
GROUPS = 8
GROUP_TOK = 2048
LMAX = 1024
CAP = 16
TOKENS = 16384
N_GRP = 8
N_EP = 16


def draw_hidden_in(key, part):
    base = jax.random.fold_in(key, 7)
    row_key, col_key, val_key = jax.random.split(base, 3)
    row_scale = jnp.exp(jax.random.uniform(row_key, (TOKENS, 1), jnp.float32, jnp.log(0.5), jnp.log(2.0)))
    entries = jnp.clip(jax.random.normal(val_key, (TOKENS, D), jnp.float32), -4.0, 4.0)
    col_scale = jnp.exp(jax.random.uniform(col_key, (1, D), jnp.float32, jnp.log(0.3), jnp.log(3.0)))
    return (entries * row_scale * col_scale).astype(jnp.bfloat16)


def projection_draw(key, salt):
    base = jax.random.fold_in(key, salt)
    entries = jnp.clip(jax.random.normal(base, (D, HEADS * HDIM), jnp.float32), -3.0, 3.0) * D ** (-0.5)
    return entries.astype(jnp.bfloat16)


def draw_w_query(key, part):
    return projection_draw(key, 11)


def draw_w_key(key, part):
    return projection_draw(key, 23)


def levels(key, dims, cuts, low, high):
    gain = 1.0
    for dim, blocks in cuts:
        heights = jax.random.uniform(jax.random.fold_in(jax.random.fold_in(key, 6), dim), (blocks,), jnp.float32, low / len(cuts), high / len(cuts))
        gain = gain * jnp.repeat(jnp.exp(heights), dims[dim] // blocks).reshape((-1,) + (1,) * (len(dims) - 1 - dim))
    return gain


def length_profile(number_of, total, most, slope):
    weights = [(1 << 20) // math.isqrt(standing ** slope) + 1 for standing in range(2, number_of + 1)]
    spare, holding = total - most - (number_of - 1), [1] * (number_of - 1)
    while spare > 0:
        candidates = [i for i in range(number_of - 1) if holding[i] < most]
        pool, budget = sum([weights[i] for i in candidates]), spare
        for i in candidates:
            more = min(most - holding[i], max(1, budget * weights[i] // pool), spare)
            holding[i] = holding[i] + more
            spare = spare - more
    return np.array([most] + holding)


def ragged(key, count, total, most, skew):
    if count == 2:
        one = jax.random.randint(key, (), max(1, total - most), min(most, total - 1) + 1)
        return jnp.stack([one, total - one])
    tallies = jnp.asarray(length_profile(count, total, most, skew), jnp.int32)
    twos = (count - 1) // 2
    giver, taker = tallies[1:1 + 2 * twos:2], tallies[2:2 + 2 * twos:2]
    slack = jnp.minimum(giver - 1, most - taker)
    moved = jax.random.randint(jax.random.fold_in(key, 1), (twos,), 0, 1 << 20) % (slack + 1)
    tallies = tallies.at[1:1 + 2 * twos:2].set(giver - moved).at[2:2 + 2 * twos:2].set(taker + moved)
    return tallies[jax.random.permutation(jax.random.fold_in(key, 2), count)]


def assign_block(rng, own, number, rows, count, top, bound, slope):
    order = jax.random.permutation(rng, count)
    packed, ordinary = portions_of(count, rows * top, bound, slope, True), portions_of(count, rows * top, bound, slope, False)
    places = jnp.arange(count)

    def named(lengths, turn):
        used = int((lengths > 0).sum())
        fixed = max(1, used // 4)
        shifted = fixed + (places - fixed + turn * (used - fixed)) % max(1, count - fixed)
        return jnp.zeros((count,), jnp.int32).at[order[jnp.where(places < fixed, places, shifted)]].set(jnp.asarray(lengths, jnp.int32))

    lengths = jnp.where(number % 4 == 0, named(packed, number // 4), named(ordinary, number - number // 4 - 1))
    mixed = jax.random.permutation(jax.random.fold_in(own, 3), count)
    giver, receiver = mixed[0:count // 2 * 2:2], mixed[1:count // 2 * 2:2]
    room = jnp.minimum(lengths[giver] - 1, bound - lengths[receiver]) // 2
    room = jnp.where((giver == order[0]) | (receiver == order[0]) | (lengths[receiver] == 0), 0, jnp.maximum(room, 0))
    shifted = jax.random.randint(jax.random.fold_in(own, 4), (count // 2,), 0, 1 << 20) % (room + 1)
    lengths = lengths.at[giver].add(-shifted).at[receiver].add(shifted)
    labels = jnp.searchsorted(jnp.cumsum(lengths), jnp.arange(rows * top), side="right").astype(jnp.int32)
    grid = labels.reshape(top, rows).T
    grid = grid[jax.random.permutation(jax.random.fold_in(own, 1), rows)]
    turn = jax.random.randint(jax.random.fold_in(own, 2), (rows, 1), 0, top)
    return jnp.take_along_axis(grid, (jnp.arange(top)[None, :] + turn) % top, axis=1)


def portions_of(count, total, most, slope, full):
    loads = [(1 << 20) // math.isqrt(rank ** slope) + 1 for rank in range(1, count + 1)]
    largest = most if full else min(most, max(-(-total // count), total * loads[0] // sum(loads)))
    least = 1 if total - largest >= count - 1 else 0
    holding, spare = [largest] + [least] * (count - 1), total - largest - least * (count - 1)
    while spare > 0:
        free = [i for i in range(1, count) if holding[i] < largest] or [i for i in range(1, count) if holding[i] < most]
        whole, remaining = sum([loads[i] for i in free]), spare
        for i in free:
            addition = min(most - holding[i], max(1, remaining * loads[i] // whole), spare)
            holding[i] = holding[i] + addition
            spare = spare - addition
    return np.array(holding)


def centred(key, extent, deviation, limit, pieces=(), kind=jnp.bfloat16):
    array = deviation * jax.random.normal(key, extent, jnp.float32)
    if pieces:
        array = array * levels(key, extent, pieces, -0.22, 0.18)
    return jnp.clip(array, -limit, limit).astype(kind)


def setup_inputs(seed: int = 0) -> dict:
    key_of = jax.random.split(jax.random.key(seed), 15)
    hidden_in = draw_hidden_in(jax.random.fold_in(key_of[14], 71), 0)
    prompt_lengths = jax.vmap(lambda own: ragged(own, PROMPTS + 1, GROUP_TOK, LMAX, 2))(jax.random.split(key_of[1], GROUPS)).reshape((GROUPS, PROMPTS + 1)).astype(jnp.int32)
    routes_keys = jax.random.split(jax.random.fold_in(key_of[2], 1), TOKENS // TOK_DEV)
    routes_turns = jax.random.permutation(jax.random.fold_in(key_of[2], 3), TOKENS // TOK_DEV)
    routes = jax.vmap(lambda own, number: assign_block(jax.random.fold_in(key_of[2], 2), own, number, TOK_DEV, EXPERTS, TOPK, CAP, 2))(routes_keys, routes_turns).reshape((TOKENS, TOPK))
    route_weights = jnp.clip(0.05 + 0.35 * jax.random.uniform(key_of[3], (TOKENS, TOPK), jnp.float32) ** levels(key_of[3], (TOKENS, TOPK), ((0, 128),), -0.2, 0.2), 0.05, 0.4)
    w_query = draw_w_query(jax.random.fold_in(key_of[14], 71), 0)
    w_key = draw_w_key(jax.random.fold_in(key_of[14], 71), 0)
    w_value = centred(key_of[6], (D, HEADS * HDIM), D ** -0.5, 0.125, ((1, 16),))
    w_out = centred(key_of[7], (HEADS * HDIM, D), (HEADS * HDIM) ** -0.5, 0.125)
    shared_gate = centred(key_of[8], (D, SHARED_FF), D ** -0.5, 0.125, ((1, 8),))
    shared_up = centred(key_of[9], (D, SHARED_FF), D ** -0.5, 0.125, ((1, 8),))
    shared_down = centred(key_of[10], (SHARED_FF, D), SHARED_FF ** -0.5, 0.109375, ((0, 8),))
    expert_gate = centred(key_of[11], (2 * EXPERTS, D, FF_E // 2), D ** -0.5, 0.125, ((0, 128),))
    expert_up = centred(key_of[12], (2 * EXPERTS, D, FF_E // 2), D ** -0.5, 0.125, ((0, 128),))
    expert_down = centred(key_of[13], (2 * EXPERTS, FF_E // 2, D), FF_E ** -0.5, 0.15625, ((0, 128),))
    return {"hidden_in": hidden_in, "prompt_lengths": prompt_lengths, "routes": routes, "route_weights": route_weights, "w_query": w_query, "w_key": w_key, "w_value": w_value, "w_out": w_out, "shared_gate": shared_gate, "shared_up": shared_up, "shared_down": shared_down, "expert_gate": expert_gate, "expert_up": expert_up, "expert_down": expert_down}


epsilon = 1e-06

def rms_rows(values):
    mean_square = lax.optimization_barrier(jnp.mean(values * values, axis=-1, keepdims=True))
    return values * lax.rsqrt(mean_square + epsilon)

def segment_ids(length_row, row_total):
    prompt_ends = jnp.cumsum(length_row[:-1])
    positions = jnp.arange(row_total, dtype=jnp.int32)
    segment = lax.optimization_barrier(jnp.sum((positions[:, None] >= prompt_ends[None, :]).astype(jnp.int32), axis=1))
    return jnp.where(segment >= length_row.shape[0] - 1, -1, segment).astype(jnp.int32)

def attend(queries, key_rows, value_rows, segment, block_rows):
    row_total, heads_here, head_dim = queries.shape
    score_scale = 1.0 / math.sqrt(head_dim)
    positions = jnp.arange(row_total, dtype=jnp.int32)

    def one_block(first_row):
        query_block = lax.dynamic_slice_in_dim(queries, first_row, block_rows, 0)
        query_pos = first_row + jnp.arange(block_rows, dtype=jnp.int32)
        query_seg = lax.dynamic_slice_in_dim(segment, first_row, block_rows, 0)
        scores = jnp.einsum('qhd,khd->hqk', query_block.astype(jnp.float32), key_rows.astype(jnp.float32)) * score_scale
        allowed = (positions[None, :] <= query_pos[:, None]) & (segment[None, :] == query_seg[:, None]) & ((query_seg[:, None] >= 0) | (positions[None, :] == query_pos[:, None]))
        scores = jnp.where(allowed[None], scores, -1e+30)
        largest = lax.optimization_barrier(jnp.max(scores, axis=2, keepdims=True))
        weights = jnp.where(allowed[None], jnp.exp(scores - largest), 0.0)
        totals = lax.optimization_barrier(jnp.sum(weights, axis=2, keepdims=True))
        attn_probs = (weights / totals).astype(jnp.bfloat16)
        mixed_rows = jnp.einsum('hqk,khd->qhd', attn_probs.astype(jnp.float32), value_rows.astype(jnp.float32))
        return mixed_rows.astype(jnp.bfloat16)
    starts = jnp.arange(row_total // block_rows, dtype=jnp.int32) * block_rows
    blocks = lax.map(one_block, starts)
    return blocks.reshape(row_total, heads_here * head_dim)

def reference(hidden_in, prompt_lengths, routes, route_weights, w_query, w_key, w_value, w_out, shared_gate, shared_up, shared_down, expert_gate, expert_up, expert_down):
    group_total = prompt_lengths.shape[0]
    row_total, width = hidden_in.shape
    group_rows = row_total // group_total
    normed = rms_rows(hidden_in.astype(jnp.float32)).astype(jnp.bfloat16)
    queries = jnp.dot(normed, w_query, preferred_element_type=jnp.float32).astype(jnp.bfloat16).reshape(group_total, group_rows, HEADS, HDIM)
    key_rows = jnp.dot(normed, w_key, preferred_element_type=jnp.float32).astype(jnp.bfloat16).reshape(group_total, group_rows, HEADS, HDIM)
    value_rows = jnp.dot(normed, w_value, preferred_element_type=jnp.float32).astype(jnp.bfloat16).reshape(group_total, group_rows, HEADS, HDIM)

    def group_attention(operands):
        group_queries, group_keys, group_values, length_row = operands
        segment = segment_ids(length_row, group_rows)
        return attend(group_queries, group_keys, group_values, segment, min(512, group_rows))
    heads_out = lax.map(group_attention, (queries, key_rows, value_rows, prompt_lengths)).reshape(row_total, HEADS * HDIM)
    residual = hidden_in.astype(jnp.float32) + jnp.dot(heads_out, w_out, preferred_element_type=jnp.float32)
    normed_moe = rms_rows(residual).astype(jnp.bfloat16)
    shared_gate_act = jnp.dot(normed_moe, shared_gate, preferred_element_type=jnp.float32)
    shared_up_act = jnp.dot(normed_moe, shared_up, preferred_element_type=jnp.float32)
    shared_hidden = (jax.nn.silu(shared_gate_act) * shared_up_act).astype(jnp.bfloat16)
    shared_out = jnp.dot(shared_hidden, shared_down, preferred_element_type=jnp.float32)
    flat_experts = routes.reshape(-1)
    route_total = flat_experts.shape[0]
    token_index = jnp.arange(route_total, dtype=jnp.int32) // TOPK
    padded_tokens = jnp.concatenate((token_index, jnp.full((1,), row_total, jnp.int32)))
    padded_weights = jnp.concatenate((route_weights.reshape(-1), jnp.zeros((1,), jnp.float32)))
    padded_rows = jnp.concatenate((normed_moe, jnp.zeros((1, width), jnp.bfloat16)), axis=0)
    slot_limit = N_GRP * N_EP * CAP

    def expert_step(carry, expert):
        chosen = flat_experts == expert
        rank_in = jnp.cumsum(chosen.astype(jnp.int32)) - 1
        slot_index = jnp.where(chosen, rank_in, slot_limit).astype(jnp.int32)
        slot_source = jnp.full((slot_limit + 1,), route_total, jnp.int32).at[slot_index].set(jnp.arange(route_total, dtype=jnp.int32))[:slot_limit]
        source_token = padded_tokens[slot_source]
        source_weight = padded_weights[slot_source]
        token_block = padded_rows[source_token]
        expert_value = jnp.zeros((slot_limit, width), jnp.float32)
        for half_index in range(2):
            row_index = (2 * expert + half_index).astype(jnp.int32)
            gate_half = lax.dynamic_index_in_dim(expert_gate, row_index, 0, keepdims=False)
            up_half = lax.dynamic_index_in_dim(expert_up, row_index, 0, keepdims=False)
            down_half = lax.dynamic_index_in_dim(expert_down, row_index, 0, keepdims=False)
            gate_act = jnp.dot(token_block, gate_half, preferred_element_type=jnp.float32)
            up_act = jnp.dot(token_block, up_half, preferred_element_type=jnp.float32)
            hidden = (jax.nn.silu(gate_act) * up_act).astype(jnp.bfloat16)
            partial_value = jnp.dot(hidden, down_half, preferred_element_type=jnp.float32).astype(jnp.bfloat16)
            expert_value = expert_value + partial_value.astype(jnp.float32)
        carry = carry.at[source_token].add(expert_value * source_weight[:, None], mode='drop')
        return (carry, None)
    routed, unused = lax.scan(expert_step, jnp.zeros((row_total, width), jnp.float32), jnp.arange(EXPERTS, dtype=jnp.int32))
    attended = residual.astype(jnp.bfloat16)
    moe_update = (shared_out + routed).astype(jnp.bfloat16)
    return (attended, moe_update)
```

```python
import math

import jax
import jax.numpy as jnp
from jax import lax
from jax.experimental import pallas as pl
from jax.experimental.pallas import tpu as pltpu
from jax.sharding import PartitionSpec as P

MESH = pl.DeviceIdType.MESH
HDIM = 128
EPS = 1e-06
SIDE = 4
F32 = jnp.float32
BF16 = jnp.bfloat16


def nt_dot(a, b):
    return lax.dot_general(a, b, (((1,), (1,)), ((), ())), preferred_element_type=F32)


def nn_dot(a, b):
    return jnp.dot(a, b, preferred_element_type=F32)


def front_kernel(
    lens, hid, wq, wk, wv, wo_hbm, att_out, nm_out,
    g, w, wo, qkv, o, h, res, w_sem, ss, rs, hs, hr,
):
    tok, width = hid.shape
    half_w = width // 2
    ep_count = SIDE * SIDE
    rows_all = tok * ep_count
    grp = lax.axis_index("grp")
    me = lax.axis_index("ep")
    x = me // SIDE
    y = lax.rem(me, SIDE)

    w_copies = [
        pltpu.make_async_copy(src, w.at[:, pl.ds(n * HDIM, HDIM)], w_sem.at[n])
        for n, src in enumerate((wq, wk, wv))
    ]
    w_copies.append(pltpu.make_async_copy(wo_hbm, wo, w_sem.at[3]))
    for c in w_copies:
        c.start()

    barrier = pltpu.get_barrier_semaphore()

    @pl.loop(1, ep_count)
    def _(k):
        pl.semaphore_signal(
            barrier, inc=1, device_id=(grp, lax.rem(me + k, ep_count)), device_id_type=MESH
        )

    hv = hid[...].astype(F32)
    scale = lax.rsqrt(jnp.mean(hv * hv, axis=-1, keepdims=True) + EPS)
    normed = (hv * scale).astype(BF16)
    own_rows = pl.ds(pl.multiple_of(me * tok, tok), tok)
    g[0, own_rows, :] = normed[:, :half_w]
    g[1, own_rows, :] = normed[:, half_w:]
    pl.semaphore_wait(barrier, ep_count - 1)

    sends = []

    def region(half, dx, dy, piece):
        src = lax.rem(x + dx, SIDE) * SIDE + lax.rem(y + dy, SIDE)
        if piece is None:
            return g.at[half, pl.ds(pl.multiple_of(src * tok, tok), tok), :]
        sub = tok // 2
        return g.at[half, pl.ds(pl.multiple_of(src * tok + sub * piece, sub), sub), :]

    def coords(half, p, q):
        return (p, q) if half == 0 else (q, p)

    def send(half, p, q, piece, first_axis, sign):
        dx, dy = coords(half, p, q)
        rp, rq = ((p - sign) % SIDE, q) if first_axis else (p, (q - sign) % SIDE)
        rdx, rdy = coords(half, rp, rq)
        along_x = first_axis == (half == 0)
        step = sign % SIDE
        if along_x:
            dest = lax.rem(x + step, SIDE) * SIDE + y
        else:
            dest = x * SIDE + lax.rem(y + step, SIDE)
        ref = region(half, dx, dy, piece)
        d = pltpu.make_async_remote_copy(
            src_ref=ref,
            dst_ref=ref,
            send_sem=ss.at[len(sends)],
            recv_sem=rs.at[half, rdx, rdy, piece or 0],
            device_id=(grp, dest),
            device_id_type=MESH,
        )
        d.start()
        sends.append(d)

    def arrive(half, p, q, piece=None):
        dx, dy = coords(half, p, q)
        ref = region(half, dx, dy, piece)
        pltpu.make_async_remote_copy(
            src_ref=ref,
            dst_ref=ref,
            send_sem=ss.at[0],
            recv_sem=rs.at[half, dx, dy, piece or 0],
            device_id=(grp, lax.rem(me + 1, ep_count)),
            device_id_type=MESH,
        ).wait_recv()

    both = (0, 1)

    def fan(half, p):
        for sign in (1, -1):
            send(half, p, 0, None, False, sign)

    for half in both:
        for sign in (1, -1):
            send(half, 0, 0, None, True, sign)
    for half in both:
        fan(half, 0)
    for half in both:
        arrive(half, 3, 0)
        send(half, 3, 0, 0, True, 1)
        arrive(half, 1, 0)
        send(half, 1, 0, 1, True, -1)
    for half in both:
        fan(half, 3)
        fan(half, 1)

    def pass_on(half, p):
        arrive(half, p, 3)
        send(half, p, 3, 0, False, 1)
        arrive(half, p, 1)
        send(half, p, 1, 1, False, -1)

    for half in both:
        pass_on(half, 0)
    for half in both:
        arrive(half, 2, 0, 0)
        arrive(half, 2, 0, 1)
        fan(half, 2)
    for half in both:
        pass_on(half, 3)
        pass_on(half, 1)

    for c in w_copies[:3]:
        c.wait()

    def project(dx):
        start = pl.multiple_of(lax.rem(x + dx, SIDE) * (SIDE * tok), SIDE * tok)
        rows = pl.ds(start, SIDE * tok)
        acc = nn_dot(g[0, rows, :], w[:half_w, :]) + nn_dot(g[1, rows, :], w[half_w:, :])
        qkv[rows, :] = acc.astype(BF16)

    arrive(0, 0, 2, 0)
    arrive(0, 0, 2, 1)
    for half in both:
        pass_on(half, 2)
    project(0)
    for dx in (3, 1):
        arrive(0, dx, 2, 0)
        arrive(0, dx, 2, 1)
        project(dx)
    for piece in both:
        arrive(0, 2, 2, piece)
        for dy in range(SIDE):
            arrive(1, dy, 2, piece)
    project(2)

    ends = [lens[0, 0]]
    for j in range(1, 4):
        ends.append(ends[-1] + lens[0, j])
    q_rows = 2 * tok
    big = SIDE * tok
    score_scale = 1.0 / math.sqrt(HDIM)
    head_sends = []
    for i in range(SIDE):
        keys = (i + 1) * big

        @pl.loop(0, big // q_rows)
        def _(r):
            row0 = pl.multiple_of(i * big + r * q_rows, q_rows)
            qb = qkv[pl.ds(row0, q_rows), :HDIM]
            s = nt_dot(qb, qkv[:keys, HDIM : 2 * HDIM]) * score_scale
            pos = row0 + lax.broadcasted_iota(jnp.int32, (q_rows, 1), 0)
            first = jnp.zeros_like(pos)
            for e in ends[:3]:
                first = jnp.where(pos >= e, e, first)
            first = jnp.where(pos >= ends[3], pos, first)
            kpos = lax.broadcasted_iota(jnp.int32, (q_rows, keys), 1)
            s = jnp.where((kpos >= first) & (kpos <= pos), s, -1e30)
            e = jnp.exp(s - jnp.max(s, axis=1, keepdims=True))
            inv = 1.0 / jnp.sum(e, axis=1, keepdims=True)
            probs = (e * inv).astype(BF16)
            o[pl.ds(row0, q_rows), :] = nn_dot(probs, qkv[:keys, 2 * HDIM :]).astype(BF16)

        for j in range(SIDE * i, SIDE * i + SIDE):
            d = pltpu.make_async_remote_copy(
                src_ref=o.at[pl.ds(j * tok, tok), :],
                dst_ref=h.at[:, pl.ds(pl.multiple_of(me * HDIM, HDIM), HDIM)],
                send_sem=hs.at[j],
                recv_sem=hr.at[me],
                device_id=(grp, j),
                device_id_type=MESH,
            )
            head_sends.append(d)

            @pl.when(me != j)
            def _():
                d.start()

    h[:, pl.ds(pl.multiple_of(me * HDIM, HDIM), HDIM)] = o[own_rows, :]
    for d in sends:
        d.wait_send()
    w_copies[3].wait()
    for j in range(ep_count):
        d = pltpu.make_async_remote_copy(
            src_ref=o.at[pl.ds(j * tok, tok), :],
            dst_ref=h.at[:, pl.ds(j * HDIM, HDIM)],
            send_sem=hs.at[j],
            recv_sem=hr.at[j],
            device_id=(grp, j),
            device_id_type=MESH,
        )

        @pl.when(me != j)
        def _():
            d.wait_send()
            d.wait_recv()

    total = jnp.zeros((tok, 1), F32)
    chunk = width // 4
    for c in range(4):
        cols = slice(c * chunk, (c + 1) * chunk)
        part = hid[:, cols].astype(F32) + nn_dot(h[...], wo[:, cols])
        res[:, cols] = part
        total = total + jnp.sum(part * part, axis=1, keepdims=True)
    scale2 = lax.rsqrt(total / width + EPS)
    att_out[...] = res[...].astype(BF16)
    nm_out[...] = (res[...] * scale2).astype(BF16)


def front(hidden_in, prompt_lengths, w_query, w_key, w_value, w_out):
    tok, width = hidden_in.shape
    rows_all = tok * SIDE * SIDE
    any_spec = pl.BlockSpec(memory_space=pl.ANY)
    vmem = pl.BlockSpec(memory_space=pltpu.VMEM)
    out = jax.ShapeDtypeStruct((tok, width), BF16)
    return pl.pallas_call(
        front_kernel,
        out_shape=(out, out),
        in_specs=[pl.BlockSpec(memory_space=pltpu.SMEM), vmem] + [any_spec] * 4,
        out_specs=(vmem, vmem),
        scratch_shapes=[
            pltpu.VMEM((2, rows_all, width // 2), BF16),
            pltpu.VMEM((width, 3 * HDIM), BF16),
            pltpu.VMEM((width, width), BF16),
            pltpu.VMEM((rows_all, 3 * HDIM), BF16),
            pltpu.VMEM((rows_all, HDIM), BF16),
            pltpu.VMEM((tok, width), BF16),
            pltpu.VMEM((tok, width), F32),
            pltpu.SemaphoreType.DMA((4,)),
            pltpu.SemaphoreType.DMA((40,)),
            pltpu.SemaphoreType.DMA((2, SIDE, SIDE, 2)),
            pltpu.SemaphoreType.DMA((SIDE * SIDE,)),
            pltpu.SemaphoreType.DMA((SIDE * SIDE,)),
        ],
        compiler_params=pltpu.CompilerParams(collective_id=0, has_side_effects=True),
        name="front",
    )(prompt_lengths, hidden_in, w_query, w_key, w_value, w_out)


def slot_matrix(routes_t, weights_t, expert_count, capacity):
    tok = routes_t.shape[1]
    experts = jnp.arange(expert_count, dtype=jnp.int32)
    hit = routes_t[:, None, :] == experts[None, :, None]
    mask = jnp.any(hit, axis=0)
    gate = jnp.sum(jnp.where(hit, weights_t[:, None, :], 0.0), axis=0)
    earlier = jnp.arange(tok)[:, None] < jnp.arange(tok)[None, :]
    rank = nn_dot(mask.astype(BF16), earlier.astype(BF16)).astype(jnp.int32)
    rank = jnp.where(mask, rank, -1)
    pick = rank[:, None, :] == jnp.arange(capacity, dtype=jnp.int32)[None, :, None]
    pick = pick.reshape(expert_count * capacity, tok)
    gates = jnp.broadcast_to(gate[:, None, :], (expert_count, capacity, tok)).reshape(pick.shape)
    return pick.astype(BF16), jnp.where(pick, gates, 0.0)


def local(
    hidden_in, prompt_lengths, routes, route_weights, w_query, w_key, w_value, w_out,
    shared_gate, shared_up, shared_down, expert_gate, expert_up, expert_down,
):
    tok_rows, width = hidden_in.shape
    device_count = lax.axis_size("grp") * lax.axis_size("ep")
    expert_count = device_count // 2
    capacity = 8 * tok_rows // expert_count
    pick, gates = slot_matrix(routes.T, route_weights.T, expert_count, capacity)
    attended, normed_moe = front(hidden_in, prompt_lengths, w_query, w_key, w_value, w_out)

    gathered = lax.all_gather(normed_moe, "grp", axis=0, tiled=True)
    gate_act = nn_dot(gathered, shared_gate)
    up_act = nn_dot(gathered, shared_up)
    hidden = (jax.nn.silu(gate_act) * up_act).astype(BF16)
    shared_out = lax.psum_scatter(
        nn_dot(hidden, shared_down).astype(BF16), "grp", scatter_dimension=0, tiled=True
    ).astype(F32)

    outbound = nn_dot(pick, normed_moe).astype(BF16).reshape(expert_count, 1, capacity, width)
    outbound = jnp.broadcast_to(outbound, (expert_count, 2, capacity, width)).reshape(
        device_count, capacity, width
    )
    received = lax.all_to_all(outbound, ("grp", "ep"), split_axis=0, concat_axis=0, tiled=True)
    flat = received.reshape(-1, width)
    act = jax.nn.silu(nn_dot(flat, expert_gate[0])) * nn_dot(flat, expert_up[0])
    parts = nn_dot(act.astype(BF16), expert_down[0]).astype(BF16).reshape(received.shape)
    returned = lax.all_to_all(parts, ("grp", "ep"), split_axis=0, concat_axis=0, tiled=True)
    both = jnp.broadcast_to(
        gates.reshape(expert_count, 1, capacity, tok_rows),
        (expert_count, 2, capacity, tok_rows),
    ).reshape(device_count * capacity, tok_rows)
    high = both.astype(BF16)
    low = (both - high.astype(F32)).astype(BF16)
    mix = jnp.concatenate((high, low), axis=1)
    sums = lax.dot_general(
        mix, returned.reshape(-1, width), (((0,), (0,)), ((), ())), preferred_element_type=F32
    )
    routed = sums[:tok_rows] + sums[tok_rows:]
    return attended, (shared_out + routed).astype(BF16)


def solution(mesh):
    in_specs = (
        P(("grp", "ep"), None),
        P("grp", None),
        P(("grp", "ep"), None),
        P(("grp", "ep"), None),
        P(None, "ep"),
        P(None, "ep"),
        P(None, "ep"),
        P(),
        P(None, "grp"),
        P(None, "grp"),
        P("grp", None),
        P(("grp", "ep"), None, None),
        P(("grp", "ep"), None, None),
        P(("grp", "ep"), None, None),
    )
    out_specs = (P(("grp", "ep"), None), P(("grp", "ep"), None))
    return jax.shard_map(local, mesh=mesh, in_specs=in_specs, out_specs=out_specs, check_vma=False)
```
